32 devices in a mesh: row: 4 (over y, core), col: 8 (over z, x).
Axes of the slice: x: 2, y: 2, z: 4, core: 2. Of those that a mesh axis runs over, the one named last changes fastest.
Arguments:
- embeddings: bfloat16 [4096, 1024], P(('row', 'col')), may hold values from -6 to 6
- labels: int32 [4096], P(('row', 'col')), may hold values from 0 to 511
- candidates: int32 [4, 8, 16], P('row', 'col'), may hold values from 0 to 32, as said below
Outputs:
- scores: float32 [4096, 256], P(('row', 'col'))
The draws below stay inside these ranges and needn't reach their ends.
Inputs may be any that keep to these rules, and one draw needn't show every extreme that they name: `candidates`: each owner's entries are distinct and ascending, the value 32 only at the end; every named pair has p < q; every tile is in at least one named pair.
All inputs are finite; a program needn't handle non-finite values.
Results may differ from the reference program's by a relative error of at most 0.0016.
Values may be sent and summed in bfloat16 or wider, within the bound.
No kernel may reach another device: no remote copies, remote signals or barrier semaphores. Data moves between devices by JAX's collectives and lax.ppermute only.
A program may use at most 64 MiB of HBM per device.

```python
import math
import jax
import jax.numpy as jnp
from jax import lax

D = 1024
LABELS = 256
TILE = 128
STEPS = 2
GRID_R = 4
GRID_C = 8
SLOTS = 32
KMAX = 16
TOTAL = 4096


def draw_candidates(key, part):
    grid_rows = GRID_R
    grid_cols = GRID_C
    owner_row = jnp.arange(grid_rows, dtype=jnp.int32)[:, None, None]
    owner_col = jnp.arange(grid_cols, dtype=jnp.int32)[None, :, None]
    codes = jnp.arange(SLOTS, dtype=jnp.int32)[None, None, :]
    first_tile = owner_row * grid_cols + codes // grid_rows
    second_tile = codes % grid_rows * grid_cols + owner_col
    is_upper = first_tile < second_tile
    is_chain = second_tile == first_tile + 1
    noise = jax.random.randint(key, (grid_rows, grid_cols, SLOTS), 0, 1 << 20, dtype=jnp.int32)
    ranked = noise * SLOTS + codes + jnp.where(is_chain, 1 << 28, 0)
    ranked = jnp.where(is_upper, ranked, -1 - codes)
    top_values, top_codes = lax.top_k(ranked, KMAX)
    chosen = jnp.where(top_values >= 0, top_codes, SLOTS)
    return jnp.sort(chosen, axis=-1).astype(jnp.int32)


def with_ends(result, key, smallest, largest):
    longest = result.shape.index(max(result.shape))
    spots = []
    for shift in (0, 1):
        where = [jax.random.randint(jax.random.fold_in(key, axis), (), 0, length) for axis, length in enumerate(result.shape)]
        where[longest] = (where[longest] + shift) % result.shape[longest]
        spots.append(tuple(where))
    return result.at[spots[0]].set(smallest).at[spots[1]].set(largest)


def steps_of(own_key, extent, pieces, least, high):
    factor_of = 1.0
    for dim, shards_of in pieces:
        steps = jax.random.uniform(jax.random.fold_in(jax.random.fold_in(own_key, 6), dim), (shards_of,), jnp.float32, least / len(pieces), high / len(pieces))
        factor_of = factor_of * jnp.repeat(jnp.exp(steps), extent[dim] // shards_of).reshape((-1,) + (1,) * (len(extent) - 1 - dim))
    return factor_of


def scatter_about(key, dims, deviation, limit, cuts=(), held_as=jnp.bfloat16):
    gain = steps_of(key, dims, cuts, -0.22, 0.18) if cuts else 1.0
    result = jax.random.normal(key, dims, jnp.float32) * deviation * gain
    return jnp.minimum(jnp.maximum(result, -limit), limit).astype(held_as)


def setup_inputs(seed: int = 0) -> dict:
    splits = jax.random.split(jax.random.key(seed), 4)
    return {
        "embeddings": scatter_about(splits[0], (TOTAL, D), 1.0, 6.0, ((0, 32),)),
        "labels": with_ends(jax.random.randint(splits[1], (TOTAL,), 0, 2 * LABELS), jax.random.fold_in(splits[1], 1), 0, (2 * LABELS) - 1).astype(jnp.int32),
        "candidates": draw_candidates(jax.random.fold_in(splits[3], 71), 0),
    }


epsilon = 1e-06
sharpness = 32.0
keep_share = 0.9

def normalize(embeddings):
    values = embeddings.astype(jnp.float32)
    factor = lax.rsqrt(lax.optimization_barrier(jnp.mean(values * values, axis=1, keepdims=True)) + epsilon)
    return (values * factor / math.sqrt(values.shape[1])).astype(jnp.bfloat16)

def reference(embeddings, labels, candidates):
    owner_count = GRID_R * GRID_C
    normed = normalize(embeddings).reshape(owner_count, TILE, D)
    entries = candidates.reshape(owner_count, KMAX)
    owners = jnp.arange(owner_count, dtype=jnp.int32)
    owner_row = owners // GRID_C
    owner_col = owners % GRID_C
    is_live = entries < SLOTS
    row_pos = jnp.minimum(entries // GRID_R, GRID_C - 1)
    col_pos = entries % GRID_R
    first_tile = (owner_row[:, None] * GRID_C + row_pos).astype(jnp.int32)
    second_tile = (col_pos * GRID_C + owner_col[:, None]).astype(jnp.int32)

    def one_owner(owner_id):
        left_rows = normed[first_tile[owner_id]].astype(jnp.float32)
        right_rows = normed[second_tile[owner_id]].astype(jnp.float32)
        products = jnp.einsum('kad,kbd->kab', left_rows, right_rows)
        kernel = jnp.exp(sharpness * products)
        return jnp.where(is_live[owner_id][:, None, None], kernel, 0.0).astype(jnp.bfloat16)
    tiles = lax.map(one_owner, owners)
    row_sums = lax.optimization_barrier(jnp.sum(tiles, axis=3, dtype=jnp.float32)).reshape(-1, TILE)
    col_sums = lax.optimization_barrier(jnp.sum(tiles, axis=2, dtype=jnp.float32)).reshape(-1, TILE)
    degree = jax.ops.segment_sum(row_sums, first_tile.reshape(-1), owner_count)
    degree = degree + jax.ops.segment_sum(col_sums, second_tile.reshape(-1), owner_count)
    inverse = lax.rsqrt(degree)[:, :, None]
    classes = jnp.arange(LABELS, dtype=jnp.int32)
    seeds = (labels.reshape(owner_count, TILE)[:, :, None] == classes[None, None, :]).astype(jnp.float32)
    labels_now = seeds
    for repeat in range(STEPS):
        scaled = (labels_now * inverse).astype(jnp.bfloat16)

        def accumulate(running, owner_id):
            tile_block = tiles[owner_id].astype(jnp.float32)
            upward = jnp.einsum('kab,kbl->kal', tile_block, scaled[second_tile[owner_id]].astype(jnp.float32))
            downward = jnp.einsum('kab,kal->kbl', tile_block, scaled[first_tile[owner_id]].astype(jnp.float32))
            running = running + jax.ops.segment_sum(upward, first_tile[owner_id], owner_count)
            running = running + jax.ops.segment_sum(downward, second_tile[owner_id], owner_count)
            return (running, None)
        summed, unused = lax.scan(accumulate, jnp.zeros((owner_count, TILE, LABELS), jnp.float32), owners)
        labels_now = keep_share * inverse * summed + (1.0 - keep_share) * seeds
    return jnp.log(1.0 + LABELS * labels_now).reshape(owner_count * TILE, LABELS)
```

```python
import math

import jax
import jax.numpy as jnp
from jax import lax
from jax.experimental import pallas as pl
from jax.experimental.pallas import tpu as pltpu
from jax.sharding import PartitionSpec as P

LABELS = 256
LANES = 128

epsilon = 1e-06
sharpness = 32.0
keep_share = 0.9

AXES = ("row", "col")
NT = (((1,), (1,)), ((), ()))
NN = (((1,), (0,)), ((), ()))


class Layout:
    def __init__(self, rows, cols):
        self.rows = rows
        self.cols = cols
        self.col_depth = cols // 2
        self.depth = rows * cols // 8

    def device(self, x, y, depth, core):
        high, low = divmod(depth, self.col_depth)
        return ((high * 2 + y) * 2 + core) * self.cols + low * 2 + x

    def pairs(self, move):
        return [
            (self.device(x, y, d, k), self.device(*move(x, y, d, k)))
            for x in range(2)
            for y in range(2)
            for d in range(self.depth)
            for k in range(2)
        ]

    def along_depth(self, step):
        return self.pairs(lambda x, y, d, k: (x, y, d ^ step, k))

    def along_x(self):
        return self.pairs(lambda x, y, d, k: (1 - x, y, d, k))

    def along_y(self):
        return self.pairs(lambda x, y, d, k: (x, 1 - y, d, k))

    def to_core(self):
        return self.pairs(lambda x, y, d, k: (x, y, d, 1 - k))

    def to_partner(self):
        return self.pairs(lambda x, y, d, k: (x ^ (1 - k), y ^ k, d, k))

    def to_partner_core(self):
        return self.pairs(lambda x, y, d, k: (x ^ (1 - k), y ^ k, d, 1 - k))

    def to_side(self):
        return self.pairs(lambda x, y, d, k: (x ^ k, y ^ (1 - k), d, k))


def send(value, pairs):
    return lax.ppermute(value, AXES, pairs)


def call(body, out_shape, *args, in_specs=None, scratch=()):
    specs = {} if in_specs is None else {"in_specs": in_specs}
    return pl.pallas_call(body, out_shape=out_shape, scratch_shapes=list(scratch), **specs)(*args)


def normalize(embeddings):
    def body(x_ref, o_ref):
        values = x_ref[...].astype(jnp.float32)
        factor = lax.rsqrt(jnp.mean(values * values, axis=1, keepdims=True) + epsilon)
        o_ref[...] = (values * factor / math.sqrt(values.shape[1])).astype(jnp.bfloat16)

    return call(body, jax.ShapeDtypeStruct(embeddings.shape, jnp.bfloat16), embeddings)


def find_mask(layout, place, entries):
    slots = 2 * layout.depth
    shift = slots.bit_length() - 1
    low_bits = layout.col_depth.bit_length() - 1
    pair_count = 4 * slots
    owners = entries.shape[0]

    def body(place_ref, e_ref, o_ref):
        x, y, deep, core = place_ref[0], place_ref[1], place_ref[2], place_ref[3]
        anti = 1 - core
        low0 = deep & (layout.col_depth - 1)
        high0 = deep >> low_bits

        def parts(shape):
            s = lax.broadcasted_iota(jnp.int32, shape, 0)
            j = s & (slots - 1)
            i = s >> shift
            d = j >> 1
            return i >> 1, i & 1, j & 1, d & (layout.col_depth - 1), d >> low_bits

        far, other, side, d_low, d_high = parts((pair_count, owners))
        at = lax.broadcasted_iota(jnp.int32, (pair_count, owners), 1)
        first = d_low + layout.depth * (side * core + 2 * far * core + 4 * other)
        second = d_high * layout.col_depth + layout.depth * (far * anti + 2 * side * anti)
        table = e_ref[...].astype(jnp.float32).astype(jnp.bfloat16)

        def pick(which):
            one = jnp.where(at == which, 1.0, 0.0).astype(jnp.bfloat16)
            return lax.dot_general(one, table, NN, preferred_element_type=jnp.float32)

        far, other, side, d_low, d_high = parts((pair_count, LANES))
        col_p = low0 * 2 + (x ^ (far * anti))
        row_p = (high0 * 2 + (y ^ (far * core))) * 2 + (core ^ other)
        col_q = (low0 ^ d_low) * 2 + (x ^ (side * core))
        row_q = ((high0 ^ d_high) * 2 + (y ^ (side * anti))) * 2 + core
        code_first = (col_p * layout.rows + row_q).astype(jnp.float32)
        code_second = (col_q * layout.rows + row_p).astype(jnp.float32)
        hit = (pick(first) == code_first) | (pick(second) == code_second)
        found = jnp.max(jnp.where(hit, 1.0, 0.0), axis=1, keepdims=True)
        o_ref[...] = jnp.broadcast_to(found, (pair_count, LANES))

    return call(
        body,
        jax.ShapeDtypeStruct((pair_count, LANES), jnp.float32),
        place,
        entries,
        in_specs=[pl.BlockSpec(memory_space=pltpu.SMEM), pl.BlockSpec(memory_space=pltpu.VMEM)],
    )


def affinities(step, slots, left, right, mask):
    tile, width = left[0].shape

    def body(a, b, c, d, e, f, m_ref, w_ref, s_ref):
        lhs = jnp.concatenate([r[...] for r in (a, b, c, d)], axis=0)
        rhs = jnp.concatenate([e[...], f[...]], axis=0)
        products = lax.dot_general(lhs, rhs, NT, preferred_element_type=jnp.float32)
        total = [jnp.zeros((1, tile), jnp.float32) for _ in range(2)]
        for i in range(4):
            for j in range(2):
                rows, cols = slice(i * tile, (i + 1) * tile), slice(j * tile, (j + 1) * tile)
                at = i * slots + 2 * step + j
                kernel = jnp.exp(sharpness * products[rows, cols])
                kept = jnp.where(m_ref[at : at + 1, :] > 0.5, kernel, 0.0).astype(jnp.bfloat16)
                w_ref[rows, cols] = kept
                total[j] += jnp.sum(kept.astype(jnp.float32), axis=0, keepdims=True)
        s_ref[...] = jnp.concatenate(total, axis=0)

    return call(
        body,
        (
            jax.ShapeDtypeStruct((4 * tile, 2 * tile), jnp.bfloat16),
            jax.ShapeDtypeStruct((2, tile), jnp.float32),
        ),
        *left,
        *right,
        mask,
    )


def add_depth(layout, parts):
    slots = 2 * layout.depth

    def body(*refs):
        out = refs[-1]
        for half in range(2):
            for d in range(layout.depth):
                total = None
                for t in range(layout.depth):
                    at = half * slots + 2 * (d ^ t)
                    rows = refs[t][at : at + 2, :]
                    total = rows if total is None else total + rows
                out[half * slots + 2 * d : half * slots + 2 * d + 2, :] = total

    return call(body, jax.ShapeDtypeStruct(parts[0].shape, jnp.float32), *parts)


def column(row):
    n = row.shape[1]
    eye = lax.broadcasted_iota(jnp.int32, (n, n), 0) == lax.broadcasted_iota(jnp.int32, (n, n), 1)
    return jnp.sum(jnp.where(eye, jnp.broadcast_to(row, (n, n)), 0.0), axis=1, keepdims=True)


def partial_shapes(tile):
    return tuple(jax.ShapeDtypeStruct((tile, LABELS), jnp.float32) for _ in range(4))


def first_step(slots, weights, near, far):
    tile = near.shape[1]

    def body(*refs):
        w_refs, (n_ref, f_ref), outs = refs[: len(weights)], refs[len(weights) : len(weights) + 2], refs[len(weights) + 2 :]
        classes = lax.broadcasted_iota(jnp.int32, (LABELS, tile), 0).astype(jnp.float32)
        total = None
        for step, w_ref in enumerate(w_refs):
            blocks = []
            for side in range(2):
                j = 2 * step + side
                o = 2 * step + 1 - side
                degree = n_ref[j : j + 1, :] + f_ref[o : o + 1, :]
                label = n_ref[slots + j : slots + j + 1, :] + f_ref[slots + o : slots + o + 1, :]
                inverse = lax.rsqrt(degree)
                blocks.append(jnp.where(classes == label, inverse, 0.0).astype(jnp.bfloat16))
                if j == 0:
                    outs[4][...] = jnp.broadcast_to(column(inverse), (tile, LANES))
                    outs[5][...] = jnp.broadcast_to(column(label), (tile, LANES))
            scaled = jnp.concatenate(blocks, axis=1)
            term = lax.dot_general(w_ref[...], scaled, NT, preferred_element_type=jnp.float32)
            total = term if total is None else total + term
        for i in range(4):
            outs[i][...] = total[i * tile : (i + 1) * tile, :]

    wide = jax.ShapeDtypeStruct((tile, LANES), jnp.float32)
    return call(body, partial_shapes(tile) + (wide, wide), *weights, near, far)


def spread_of(part_refs, i_ref, l_ref):
    summed = (part_refs[0][...] + part_refs[1][...]) + (part_refs[2][...] + part_refs[3][...])
    inverse = i_ref[:, :1]
    classes = lax.broadcasted_iota(jnp.int32, summed.shape, 1).astype(jnp.float32)
    seeds = jnp.where(l_ref[:, :1] == classes, 1.0, 0.0)
    return keep_share * inverse * summed + (1.0 - keep_share) * seeds, inverse


def rescale(parts, inverse, label):
    def body(a, b, c, d, i_ref, l_ref, o_ref):
        now, factor = spread_of((a, b, c, d), i_ref, l_ref)
        o_ref[...] = (now * factor).astype(jnp.bfloat16)

    return call(body, jax.ShapeDtypeStruct(parts[0].shape, jnp.bfloat16), *parts, inverse, label)


def scores_of(parts, inverse, label):
    def body(a, b, c, d, i_ref, l_ref, o_ref):
        now, _ = spread_of((a, b, c, d), i_ref, l_ref)
        o_ref[...] = jnp.log(1.0 + LABELS * now)

    return call(body, jax.ShapeDtypeStruct(parts[0].shape, jnp.float32), *parts, inverse, label)


def second_step(weights, own, near):
    tile = own[0].shape[0]
    count = len(weights)

    def body(*refs):
        w_refs, a_refs, b_refs, outs = refs[:count], refs[count : 2 * count], refs[2 * count : 3 * count], refs[3 * count :]
        total = None
        for w_ref, a_ref, b_ref in zip(w_refs, a_refs, b_refs):
            rhs = jnp.concatenate([a_ref[...], b_ref[...]], axis=0)
            term = lax.dot_general(w_ref[...], rhs, NN, preferred_element_type=jnp.float32)
            total = term if total is None else total + term
        for i in range(4):
            outs[i][...] = total[i * tile : (i + 1) * tile, :]

    return call(body, partial_shapes(tile), *weights, *own, *near)


def exchange(layout, parts):
    return [
        parts[0],
        send(parts[1], layout.to_core()),
        send(parts[2], layout.to_partner()),
        send(parts[3], layout.to_partner_core()),
    ]


def over_depth(layout, value):
    pieces = [value]
    width = 1
    while width < layout.depth:
        pieces = pieces + [send(piece, layout.along_depth(width)) for piece in pieces]
        width *= 2
    return pieces


def on_device(layout, embeddings, labels, candidates):
    tile = embeddings.shape[0]
    depth, slots = layout.depth, 2 * layout.depth
    row, col = lax.axis_index("row"), lax.axis_index("col")
    place = jnp.stack(
        [
            col % 2,
            (row // 2) % 2,
            (row // 4) * layout.col_depth + col // 2,
            row % 2,
        ]
    ).astype(jnp.int32)

    normed = normalize(embeddings)
    along = over_depth(layout, normed)
    across = [send(piece, layout.to_side()) for piece in along]
    left = [
        normed,
        send(normed, layout.to_core()),
        send(normed, layout.to_partner()),
        send(across[0], layout.to_core()),
    ]

    entries = jnp.pad(candidates.reshape(1, -1), ((0, 0), (0, LANES - candidates.shape[-1])), constant_values=-1)
    moves = [layout.along_depth(1 << s) for s in range(depth.bit_length() - 1)]
    for move in moves + [layout.along_x(), layout.along_y(), layout.to_core()]:
        entries = jnp.concatenate([entries, send(entries, move)], axis=0)
    mask = find_mask(layout, place, entries)

    weights, sums = [], []
    for step in range(depth):
        block, total = affinities(step, slots, left, (along[step], across[step]), mask)
        weights.append(block)
        sums.append(total)

    mine = jnp.pad(labels.astype(jnp.float32)[None, :], ((0, slots - 1), (0, 0)))
    message = jnp.concatenate(sums + [mine], axis=0)
    near = add_depth(layout, [message] + [send(message, layout.along_depth(t)) for t in range(1, depth)])
    far = send(near, layout.to_side())

    *parts, inverse, label = first_step(slots, weights, near, far)
    scaled = rescale(exchange(layout, parts), inverse, label)
    own = over_depth(layout, scaled)
    parts = second_step(weights, own, [send(piece, layout.to_side()) for piece in own])
    return scores_of(exchange(layout, parts), inverse, label)


def solution(mesh):
    layout = Layout(mesh.shape["row"], mesh.shape["col"])

    def body(embeddings, labels, candidates):
        return on_device(layout, embeddings, labels, candidates)

    return jax.shard_map(
        body,
        mesh=mesh,
        in_specs=(P(("row", "col"), None), P(("row", "col")), P("row", "col", None)),
        out_specs=P(("row", "col"), None),
        check_vma=False,
    )
```
